32 devices in a mesh: group: 8 (over z, x), shard: 4 (over y, core).
Axes of the slice: x: 2, y: 2, z: 4, core: 2. Of those that a mesh axis runs over, the one named last changes fastest.
Arguments:
- inputs: bfloat16 [2, 8, 1024, 768], P(None, 'group', 'shard'), may hold values from -6 to 6
- block_ids: int32 [2, 8, 1024], P(None, 'group'), may hold values from 0 to 7, never falling along the last dimension, each value on 1 to 256 neighbouring positions
- attn_gain: bfloat16 [768], P('shard'), may hold values from 0.099609375 to 1.8984375
- attn_shift: bfloat16 [768], P('shard'), may hold values from -2 to 2
- weight_qkv: bfloat16 [768, 2304], P('shard'), may hold values from -0.3125 to 0.3125
- bias_qv: bfloat16 [1536], P('shard'), may hold values from -2 to 2
- weight_out: bfloat16 [768, 768], P('shard'), may hold values from -3.5 to 3.5
- bias_out: bfloat16 [768], P('shard'), may hold values from -5 to 5
- mlp_gain: bfloat16 [768], P('shard'), may hold values from 0.099609375 to 1.8984375
- mlp_shift: bfloat16 [768], P('shard'), may hold values from -2 to 2
- weight_up: bfloat16 [768, 3072], P('shard'), may hold values from -0.21875 to 0.21875
- bias_up: bfloat16 [3072], P('shard'), may hold values from -2 to 2
- weight_down: bfloat16 [3072, 768], P('shard'), may hold values from -0.75 to 0.75
- bias_down: bfloat16 [768], P('shard'), may hold values from -5 to 5
- cotangent: bfloat16 [2, 8, 1024, 768], P(None, 'group', 'shard'), may hold values from -6 to 6
Outputs:
- outputs: bfloat16 [2, 8, 1024, 768], P(None, 'group', 'shard')
- grad_inputs: float32 [2, 8, 1024, 768], P(None, 'group', 'shard')
- grad_attn_gain: float32 [768], P('shard')
- grad_attn_shift: float32 [768], P('shard')
- grad_weight_qkv: float32 [768, 2304], P('shard')
- grad_bias_qv: float32 [1536], P('shard')
- grad_weight_out: float32 [768, 768], P('shard')
- grad_bias_out: float32 [768], P('shard')
- grad_mlp_gain: float32 [768], P('shard')
- grad_mlp_shift: float32 [768], P('shard')
- grad_weight_up: float32 [768, 3072], P('shard')
- grad_bias_up: float32 [3072], P('shard')
- grad_weight_down: float32 [3072, 768], P('shard')
- grad_bias_down: float32 [768], P('shard')
The draws below stay inside these ranges and needn't reach their ends.
Inputs may be any that keep to these rules, and one draw needn't show every extreme that they name: `block_ids`: along each sequence the block ids never fall; each id holds 1 to 256 consecutive positions.
All inputs are finite; a program needn't handle non-finite values.
Results may differ from the reference program's by a relative error of at most 0.017.
The reference program's roundings to bfloat16 on the way count: a program that leaves them out, or rounds other values in their place, can miss the bound.
Values may be sent and summed in bfloat16 or wider, within the bound.
No kernel may reach another device: no remote copies, remote signals or barrier semaphores. Data moves between devices by JAX's collectives and lax.ppermute only.
A program may use at most 192 MiB of HBM per device.

```python
import math
import jax
import jax.numpy as jnp
import numpy as np
from jax import lax

D = 768
HEADS = 12
FF = 3072
DEPTH = 48
BLK = 256
MICRO = 2
LENGTH = 1024
SEGMENTS = 8
SEQ_TOTAL = 8
TOKENS = 16384


def level_of(stream_key, dims, cuts, smallest, high):
    level = 1.0
    for dim, shards_of in cuts:
        steps = jax.random.uniform(jax.random.fold_in(jax.random.fold_in(stream_key, 6), dim), (shards_of,), jnp.float32, smallest / len(cuts), high / len(cuts))
        level = level * jnp.repeat(jnp.exp(steps), dims[dim] // shards_of).reshape((-1,) + (1,) * (len(dims) - 1 - dim))
    return level


def split_up(amount, total, limit, skew):
    portions = [(1 << 20) // math.isqrt(rank ** skew) + 1 for rank in range(2, amount + 1)]
    surplus, holding = total - limit - (amount - 1), [1] * (amount - 1)
    while surplus > 0:
        free = [i for i in range(amount - 1) if holding[i] < limit]
        whole, budget = sum([portions[i] for i in free]), surplus
        for i in free:
            more = min(limit - holding[i], max(1, budget * portions[i] // whole), surplus)
            holding[i] = holding[i] + more
            surplus = surplus - more
    return np.array([limit] + holding)


def ragged(own_key, number_of, total, bound, lean):
    if number_of == 2:
        one = jax.random.randint(own_key, (), max(1, total - bound), min(bound, total - 1) + 1)
        return jnp.stack([one, total - one])
    sizes = jnp.asarray(split_up(number_of, total, bound, lean), jnp.int32)
    couples = (number_of - 1) // 2
    donor, taker = sizes[1:1 + 2 * couples:2], sizes[2:2 + 2 * couples:2]
    margin = jnp.minimum(donor - 1, bound - taker)
    passed = jax.random.randint(jax.random.fold_in(own_key, 1), (couples,), 0, 1 << 20) % (margin + 1)
    sizes = sizes.at[1:1 + 2 * couples:2].set(donor - passed).at[2:2 + 2 * couples:2].set(taker + passed)
    return sizes[jax.random.permutation(jax.random.fold_in(own_key, 2), number_of)]


def gaussian(key, dims, scale, reach, cuts=(), held_as=jnp.bfloat16):
    entries = scale * jax.random.normal(key, dims, jnp.float32)
    if cuts:
        entries = entries * level_of(key, dims, cuts, -0.22, 0.18)
    return jnp.clip(entries, -reach, reach).astype(held_as)


def setup_inputs(seed: int = 0) -> dict:
    keys = jax.random.split(jax.random.key(seed), 16)
    return {
        "inputs": gaussian(keys[0], (MICRO, SEQ_TOTAL, LENGTH, D), 1.0, 6.0, ((1, 8), (2, 4))),
        "block_ids": jax.vmap(lambda own: jnp.searchsorted(jnp.cumsum(ragged(own, SEGMENTS, LENGTH, BLK, 0)), jnp.arange(LENGTH), side="right"))(jax.random.split(keys[1], MICRO * SEQ_TOTAL)).reshape((MICRO, SEQ_TOTAL, LENGTH)).astype(jnp.int32),
        "attn_gain": jnp.clip(1.0 + 0.18 * jax.random.normal(keys[2], (D,), jnp.float32), 0.099609375, 1.8984375).astype(jnp.bfloat16),
        "attn_shift": gaussian(keys[3], (D,), 0.3, 2.0, ((0, 4),)),
        "weight_qkv": gaussian(keys[4], (D, 3 * D), (D // 2) ** -0.5, 0.3125, ((0, 4),)),
        "bias_qv": gaussian(keys[5], (2 * D,), 0.3, 2.0, ((0, 4),)),
        "weight_out": gaussian(keys[6], (D, D), (max(D // 256, 1)) ** -0.5, 3.5, ((0, 4),)),
        "bias_out": gaussian(keys[7], (D,), 1.0, 5.0, ((0, 4),)),
        "mlp_gain": jnp.clip(1.0 + 0.18 * jax.random.normal(keys[8], (D,), jnp.float32), 0.099609375, 1.8984375).astype(jnp.bfloat16),
        "mlp_shift": gaussian(keys[9], (D,), 0.3, 2.0, ((0, 4),)),
        "weight_up": gaussian(keys[10], (D, FF), D ** -0.5, 0.21875, ((0, 4),)),
        "bias_up": gaussian(keys[11], (FF,), 0.3, 2.0, ((0, 4),)),
        "weight_down": gaussian(keys[12], (FF, D), (FF // 48) ** -0.5, 0.75, ((0, 4),)),
        "bias_down": gaussian(keys[13], (D,), 1.0, 5.0, ((0, 4),)),
        "cotangent": gaussian(keys[14], (MICRO, SEQ_TOTAL, LENGTH, D), 1.0, 6.0, ((1, 8), (2, 4))),
    }


@jax.custom_vjp
def low(v):
    return lax.optimization_barrier(v.astype(jnp.bfloat16)).astype(jnp.float32)

@jax.custom_vjp
def low_back(v):
    return v

def low_keep(v):
    return (low(v), None)

def low_pass(kept, grad):
    return (grad,)

def back_keep(v):
    return (v, None)

def back_low(kept, grad):
    return (low(grad),)
low.defvjp(low_keep, low_pass)
low_back.defvjp(back_keep, back_low)

def norm_rows(rows_in, gain_in, shift_in):
    center = lax.optimization_barrier(jnp.mean(rows_in, axis=-1, keepdims=True))
    deviate = rows_in - center
    spread = lax.optimization_barrier(jnp.mean(deviate * deviate, axis=-1, keepdims=True))
    return deviate * lax.rsqrt(spread + 1e-05) * gain_in + shift_in

def gelu_tanh(rows_in):
    return 0.5 * rows_in * (1.0 + jnp.tanh(0.7978845608028654 * (rows_in + 0.044715 * rows_in * rows_in * rows_in)))

def layer(tokens, block_rows, params):
    gain_one, shift_one, mixing_weight, bias_pair, attention_weight, attention_bias, gain_two, shift_two, inner_layer_weight, inner_layer_bias, closing_weight, closing_bias = params
    highest_precision = lax.Precision.HIGHEST
    seq_count, seq_length, features = tokens.shape
    head_width = features // HEADS
    scaling = 1.0 / math.sqrt(head_width)
    branch = 1.0 / math.sqrt(DEPTH)
    opening_input = low(norm_rows(tokens, gain_one, shift_one))
    complete_bias = jnp.concatenate([bias_pair[:features], jnp.zeros((features,), jnp.float32), bias_pair[features:]])
    query_key_value_mixed = jnp.einsum('gjr,rq->gjq', opening_input, mixing_weight, precision=highest_precision) + complete_bias
    query_heads = low_back(low(query_key_value_mixed[..., :features])).reshape(seq_count, seq_length, HEADS, head_width)
    key_heads = low_back(low(query_key_value_mixed[..., features:2 * features])).reshape(seq_count, seq_length, HEADS, head_width)
    value_heads = low_back(low(query_key_value_mixed[..., 2 * features:])).reshape(seq_count, seq_length, HEADS, head_width)
    scores = jnp.einsum('sqhc,skhc->shqk', query_heads, key_heads, precision=highest_precision) * scaling
    allowed = block_rows[:, None, :] <= block_rows[:, :, None]
    scores = low_back(jnp.where(allowed[:, None, :, :], scores, -1e+30))
    prob_low = low(jax.nn.softmax(scores, axis=-1))
    attention_mixed = jnp.einsum('shqk,skhc->sqhc', prob_low, value_heads, precision=highest_precision).reshape(seq_count, seq_length, features)
    attention_mixed = low_back(low(attention_mixed))
    attention_output = low_back(jnp.einsum('gjr,rq->gjq', attention_mixed, attention_weight, precision=highest_precision) + attention_bias)
    residual = tokens + branch * attention_output
    second_output = low(norm_rows(residual, gain_two, shift_two))
    preactivation = low_back(jnp.einsum('bgj,jy->bgy', second_output, inner_layer_weight, precision=highest_precision) + inner_layer_bias)
    hidden_units = low(gelu_tanh(preactivation))
    closing_output = low_back(jnp.einsum('erv,vj->erj', hidden_units, closing_weight, precision=highest_precision) + closing_bias)
    return residual + branch * closing_output

def reference(inputs, block_ids, attn_gain, attn_shift, weight_qkv, bias_qv, weight_out, bias_out, mlp_gain, mlp_shift, weight_up, bias_up, weight_down, bias_down, cotangent):
    params = tuple((member.astype(jnp.float32) for member in (attn_gain, attn_shift, weight_qkv, bias_qv, weight_out, bias_out, mlp_gain, mlp_shift, weight_up, bias_up, weight_down, bias_down)))
    total_seqs = MICRO * SEQ_TOTAL
    per_step = math.gcd(total_seqs, 4)
    tokens = inputs.astype(jnp.float32).reshape(total_seqs // per_step, per_step, LENGTH, D)
    blocks = block_ids.reshape(total_seqs // per_step, per_step, LENGTH)
    cot_rows = cotangent.astype(jnp.float32).reshape(total_seqs // per_step, per_step, LENGTH, D)
    checked = jax.checkpoint(layer)

    def whole(tokens_all, params_all):

        def advance(carry_in, pieces):
            return (carry_in, checked(pieces[0], pieces[1], params_all))
        _, results = lax.scan(advance, jnp.zeros((), jnp.float32), (tokens_all, blocks))
        return results
    results, pullback = jax.vjp(whole, tokens, params)
    grad_tokens, grad_params = pullback(cot_rows)
    factor = 1.0 / math.sqrt(TOKENS)
    scaled = [member * factor for member in grad_params]
    return (results.astype(jnp.bfloat16).reshape(inputs.shape), grad_tokens.reshape(inputs.shape), scaled[0], scaled[1], scaled[2], scaled[3], scaled[4], scaled[5], scaled[6], scaled[7], scaled[8], scaled[9], scaled[10], scaled[11])
```

```python
import functools
import math

import jax
import jax.numpy as jnp
from jax import lax
from jax.experimental import pallas as pl
from jax.experimental.pallas import tpu as pltpu
from jax.sharding import PartitionSpec as P

HEADS = 12
DEPTH = 48
PAIR = 128
NN = (((1,), (0,)), ((), ()))
NT = (((1,), (1,)), ((), ()))
TN = (((0,), (0,)), ((), ()))
F32 = jnp.float32
BF16 = jnp.bfloat16


def dot(a, b, dims):
    return lax.dot_general(a, b, dims, preferred_element_type=F32)


def swap_core(x):
    return lax.ppermute(x, "shard", [(s, s ^ 1) for s in range(4)])


def swap_y(x):
    return lax.ppermute(x, "shard", [(s, s ^ 2) for s in range(4)])


def swap_group(x, bit):
    n = lax.axis_size("group")
    return lax.ppermute(x, "group", [(g, g ^ bit) for g in range(n)])


def gather_shard(piece, y, c):
    other = swap_y(piece)
    pair = jnp.where(y == 0, jnp.stack([piece, other]), jnp.stack([other, piece]))
    remote = swap_core(pair)
    first = jnp.where(c == 0, pair, remote)
    second = jnp.where(c == 0, remote, pair)
    return jnp.stack([first, second], axis=1).reshape((4,) + piece.shape)


def pick(x, index, axis):
    return lax.dynamic_index_in_dim(x, index, axis, keepdims=False)


def halves(x, index):
    rows = x.shape[0] // 2
    keep = lax.dynamic_slice_in_dim(x, index * rows, rows, 0)
    send = lax.dynamic_slice_in_dim(x, (1 - index) * rows, rows, 0)
    return keep, send


def reduce_all(full, y, c, group):
    n = lax.axis_size("group")
    full = full.reshape((2, 2) + full.shape[1:])
    held = (pick(full, c, 1).astype(F32) + swap_core(pick(full, 1 - c, 1)).astype(F32)).astype(BF16)
    held = (pick(held, y, 0).astype(F32) + swap_y(pick(held, 1 - y, 0)).astype(F32)).astype(BF16)
    bits = []
    bit = 1
    while bit < n:
        bits.append(bit)
        bit *= 2
    for bit in bits:
        keep, send = halves(held, (group // bit) % 2)
        held = (keep.astype(F32) + swap_group(send, bit).astype(F32)).astype(BF16)
    for bit in reversed(bits):
        other = swap_group(held, bit)
        mine = (group // bit) % 2 == 0
        held = jnp.where(
            mine, jnp.concatenate([held, other], axis=0), jnp.concatenate([other, held], axis=0)
        )
    return held.astype(F32)


def bias_of(qid, kid):
    return jnp.where(kid <= qid, 0.0, -1e30).astype(F32)


def column(row):
    n = row.shape[1]
    return jnp.transpose(jnp.broadcast_to(row, (PAIR, n)))[:, 0:1]


def head_lanes(shape, head):
    lane = lax.broadcasted_iota(jnp.int32, shape, len(shape) - 1)
    return (lane < 64) if head == 0 else (lane >= 64)


def attend_kernel(ids_ref, q_ref, k_ref, kr_ref, v_ref, vr_ref, o_ref, plo_ref, phi_ref, blo, bhi):
    blk = q_ref.shape[0] // 2

    @pl.when(pl.program_id(0) == 0)
    def _():
        own0, own1 = ids_ref[0:1, :], ids_ref[1:2, :]
        rem0, rem1 = ids_ref[2:3, :], ids_ref[3:4, :]
        q0, q1 = column(own0), column(own1)
        blo[...] = jnp.concatenate([bias_of(q0, k) for k in (own0, rem0, rem1)], axis=1)
        bhi[...] = jnp.concatenate([bias_of(q1, k) for k in (own0, rem0, rem1, own1)], axis=1)

    keys = [k_ref[0:blk, :], kr_ref[0:blk, :], kr_ref[blk:, :], k_ref[blk:, :]]
    vals = [v_ref[0:blk, :], vr_ref[0:blk, :], vr_ref[blk:, :], v_ref[blk:, :]]
    for half, (bias, count, p_ref) in enumerate(((blo, 3, plo_ref), (bhi, 4, phi_ref))):
        q = q_ref[half * blk : (half + 1) * blk, :] * BF16(0.125)
        outs = []
        for head in range(2):
            qh = jnp.where(head_lanes(q.shape, head), q, BF16(0))
            s = jnp.concatenate([dot(qh, keys[j], NT) for j in range(count)], axis=1) + bias[...]
            e = jnp.exp(s - jnp.max(s, axis=1, keepdims=True))
            p = (e * (1.0 / jnp.sum(e, axis=1, keepdims=True))).astype(BF16)
            p_ref[head] = p
            acc = None
            for j in range(count):
                t = dot(p[:, j * blk : (j + 1) * blk], vals[j], NN)
                acc = t if acc is None else acc + t
            outs.append(acc)
        o = jnp.where(head_lanes(outs[0].shape, 0), outs[0], outs[1])
        o_ref[half * blk : (half + 1) * blk, :] = o.astype(BF16)


def attend(ids, q, kv, kv_rem):
    rows, feats = q.shape
    blk = rows // 2
    pairs = feats // PAIR
    col = lambda off: pl.BlockSpec((rows, PAIR), lambda i, off=off: (0, i + off))
    return pl.pallas_call(
        attend_kernel,
        grid=(pairs,),
        in_specs=[
            pl.BlockSpec((4, blk), lambda i: (0, 0)),
            col(0),
            col(0),
            col(0),
            col(pairs),
            col(pairs),
        ],
        out_specs=[
            col(0),
            pl.BlockSpec((2, blk, 3 * blk), lambda i: (i, 0, 0)),
            pl.BlockSpec((2, blk, 4 * blk), lambda i: (i, 0, 0)),
        ],
        out_shape=[
            jax.ShapeDtypeStruct((rows, feats), BF16),
            jax.ShapeDtypeStruct((2 * pairs, blk, 3 * blk), BF16),
            jax.ShapeDtypeStruct((2 * pairs, blk, 4 * blk), BF16),
        ],
        scratch_shapes=[pltpu.VMEM((blk, 3 * blk), F32), pltpu.VMEM((blk, 4 * blk), F32)],
        cost_estimate=pl.CostEstimate(
            flops=4 * 7 * blk * blk * feats * 4, transcendentals=7 * blk * blk * 12, bytes_accessed=20 << 20
        ),
        name="attend",
    )(ids, q, kv, kv_rem, kv, kv_rem)


def attend_back_kernel(
    q_ref, k_ref, kr_ref, v_ref, vr_ref, o_ref, g_ref, plo_ref, phi_ref,
    dq_ref, dk_ref, dv_ref, dkr_ref, dvr_ref, acc_k, acc_v,
):
    blk = q_ref.shape[0] // 2
    keys = [k_ref[0:blk, :], kr_ref[0:blk, :], kr_ref[blk:, :], k_ref[blk:, :]]
    vals = [v_ref[0:blk, :], vr_ref[0:blk, :], vr_ref[blk:, :], v_ref[blk:, :]]
    for half, (count, p_ref) in enumerate(((3, plo_ref), (4, phi_ref))):
        span = slice(half * blk, (half + 1) * blk)
        q = q_ref[span, :] * BF16(0.125)
        g = g_ref[span, :]
        og = o_ref[span, :].astype(F32) * g.astype(F32)
        dqs = []
        terms_k = [[] for _ in range(count)]
        terms_v = [[] for _ in range(count)]
        for head in range(2):
            lanes = head_lanes(q.shape, head)
            gh = jnp.where(lanes, g, BF16(0))
            inner = jnp.sum(jnp.where(lanes, og, 0.0), axis=1, keepdims=True)
            acc = None
            for j in range(count):
                p = p_ref[head, :, j * blk : (j + 1) * blk]
                dp = dot(gh, vals[j], NT)
                ds = (p.astype(F32) * (dp - inner)).astype(BF16)
                t = dot(ds, keys[j], NN)
                acc = t if acc is None else acc + t
                terms_k[j].append(dot(ds, q, TN))
                terms_v[j].append(dot(p, g, TN))
            dqs.append(acc)
        lanes = head_lanes(dqs[0].shape, 0)
        dq_ref[span, :] = (jnp.where(lanes, dqs[0], dqs[1]) * 0.125).astype(BF16)
        for j in range(count):
            place = slice(j * blk, (j + 1) * blk)
            tk = jnp.where(lanes, terms_k[j][0], terms_k[j][1])
            tv = jnp.where(lanes, terms_v[j][0], terms_v[j][1])
            if half == 0:
                acc_k[place, :] = tk
                acc_v[place, :] = tv
            elif j == 3:
                dk_ref[blk:, :] = tk.astype(dk_ref.dtype)
                dv_ref[blk:, :] = tv.astype(dv_ref.dtype)
            else:
                tk = acc_k[place, :] + tk
                tv = acc_v[place, :] + tv
                if j == 0:
                    dk_ref[0:blk, :] = tk.astype(dk_ref.dtype)
                    dv_ref[0:blk, :] = tv.astype(dv_ref.dtype)
                else:
                    spot = slice((j - 1) * blk, j * blk)
                    dkr_ref[spot, :] = tk.astype(dkr_ref.dtype)
                    dvr_ref[spot, :] = tv.astype(dvr_ref.dtype)


def attend_back(q, kv, kv_rem, o, g, plo, phi):
    rows, feats = q.shape
    blk = rows // 2
    pairs = feats // PAIR
    col = lambda off: pl.BlockSpec((rows, PAIR), lambda i, off=off: (0, i + off))
    wide = jax.ShapeDtypeStruct((rows, feats), F32)
    low = jax.ShapeDtypeStruct((rows, feats), BF16)
    return pl.pallas_call(
        attend_back_kernel,
        grid=(pairs,),
        in_specs=[
            col(0), col(0), col(0), col(pairs), col(pairs), col(0), col(0),
            pl.BlockSpec((2, blk, 3 * blk), lambda i: (i, 0, 0)),
            pl.BlockSpec((2, blk, 4 * blk), lambda i: (i, 0, 0)),
        ],
        out_specs=[col(0)] * 5,
        out_shape=[low, wide, wide, low, low],
        scratch_shapes=[pltpu.VMEM((3 * blk, PAIR), F32), pltpu.VMEM((3 * blk, PAIR), F32)],
        cost_estimate=pl.CostEstimate(
            flops=8 * 7 * blk * blk * feats * 4, transcendentals=0, bytes_accessed=24 << 20
        ),
        name="attend_back",
    )(q, kv, kv_rem, kv, kv_rem, o, g, plo, phi)


def norm_rows(rows_in, gain_in, shift_in):
    center = jnp.mean(rows_in, axis=-1, keepdims=True)
    deviate = rows_in - center
    spread = jnp.mean(deviate * deviate, axis=-1, keepdims=True)
    return deviate * lax.rsqrt(spread + 1e-05) * gain_in + shift_in


def gelu_tanh(rows_in):
    return (
        0.5
        * rows_in
        * (1.0 + jnp.tanh(0.7978845608028654 * (rows_in + 0.044715 * rows_in * rows_in * rows_in)))
    )


def body(
    inputs, block_ids, attn_gain, attn_shift, weight_qkv, bias_qv, weight_out, bias_out,
    mlp_gain, mlp_shift, weight_up, bias_up, weight_down, bias_down, cotangent,
):
    micro_count, seq_count, blk, feats = inputs.shape
    seq_length = block_ids.shape[2]
    shard = lax.axis_index("shard")
    group = lax.axis_index("group")
    groups = lax.axis_size("group")
    y, c = shard // 2, shard % 2
    ff = 4 * weight_down.shape[0]
    branch = 1.0 / math.sqrt(DEPTH)
    grad_factor = 1.0 / math.sqrt(micro_count * seq_count * seq_length * groups)

    def swap_in(x):
        own = pick(x, y, 0)[0]
        other = swap_y(pick(x, 1 - y, 0)[0])
        return jnp.where(y == 0, jnp.concatenate([own, other]), jnp.concatenate([other, own]))

    def swap_out(rows):
        low, high = rows[:blk], rows[blk:]
        keep = jnp.where(y == 0, low, high)
        other = swap_y(jnp.where(y == 0, high, low))
        return jnp.where(y == 0, jnp.stack([keep, other]), jnp.stack([other, keep]))[:, None]

    vectors = (attn_gain, attn_shift, bias_qv, bias_out, mlp_gain, mlp_shift, bias_up, bias_down)
    sizes = [v.shape[0] for v in vectors]
    width = weight_qkv.shape[1]
    packed = jnp.concatenate(vectors)
    rows_v = -(-packed.shape[0] // width)
    packed = jnp.pad(packed, (0, rows_v * width - packed.shape[0])).reshape(rows_v, width)
    first_pack = jnp.concatenate([weight_qkv, jnp.pad(packed, ((0, 8 - rows_v), (0, 0)))], axis=0)
    x = swap_in(inputs)
    pack_a = gather_shard(first_pack, y, c)
    slice_rows = weight_qkv.shape[0]
    w_qkv = pack_a[:, :slice_rows].reshape(feats, width)
    vec_rows = pack_a[:, slice_rows : slice_rows + rows_v].reshape(4, rows_v * width).astype(F32)
    full_vectors = []
    at = 0
    for size in sizes:
        full_vectors.append(vec_rows[:, at : at + size].reshape(4 * size))
        at += size
    ga, sa, bqv, bo, gm, sm, bu, bd = full_vectors
    pack_b = gather_shard(jnp.concatenate([weight_out, weight_up], axis=1), y, c)
    w_out = pack_b[:, :, :feats].reshape(feats, feats)
    w_up = pack_b[:, :, feats:].reshape(feats, ff)
    w_down = gather_shard(weight_down, y, c).reshape(ff, feats)
    cot = swap_in(cotangent)

    ids_seq = pick(block_ids, y, 0)[0].astype(F32).reshape(4, blk)
    order = jnp.where(c == 0, jnp.array([0, 2, 1, 3]), jnp.array([1, 3, 0, 2]))
    ids = jnp.concatenate([pick(ids_seq, order[i], 0)[None] for i in range(4)], axis=0)

    tokens = x.astype(F32)
    first = norm_rows(tokens, ga, sa).astype(BF16)
    full_bias = jnp.concatenate([bqv[:feats], jnp.zeros((feats,), F32), bqv[feats:]])
    mixed = (jnp.dot(first, w_qkv, preferred_element_type=F32) + full_bias).astype(BF16)
    q, kv = mixed[:, :feats], mixed[:, feats:]
    kv_rem = swap_core(kv)
    attended, plo, phi = attend(ids, q, kv, kv_rem)
    residual = tokens + branch * (jnp.dot(attended, w_out, preferred_element_type=F32) + bo)
    second = norm_rows(residual, gm, sm).astype(BF16)
    pre = jnp.dot(second, w_up, preferred_element_type=F32) + bu
    hidden = gelu_tanh(pre).astype(BF16)
    closing = jnp.dot(hidden, w_down, preferred_element_type=F32) + bd
    out_rows = (residual + branch * closing).astype(BF16)
    outputs = swap_out(out_rows)

    gout = cot.astype(F32)
    g_final = (branch * gout).astype(BF16)
    gw_down = dot(hidden, g_final, TN).astype(BF16)
    own_down = reduce_all(gw_down.reshape(4, ff // 4, feats), y, c, group)
    _, gelu_pull = jax.vjp(gelu_tanh, pre)
    g_pre = gelu_pull(dot(g_final, w_down, NT))[0].astype(BF16)
    gw_up = dot(second, g_pre, TN).astype(BF16)
    g_second = dot(g_pre, w_up, NT)
    _, norm_pull = jax.vjp(norm_rows, residual, gm, sm)
    g_res_part, g_gm, g_sm = norm_pull(g_second)
    g_res = gout + g_res_part
    g_attn = (branch * g_res).astype(BF16)
    gw_out = dot(attended, g_attn, TN).astype(BF16)
    own_mid = reduce_all(
        jnp.concatenate(
            [gw_out.reshape(4, slice_rows, feats), gw_up.reshape(4, slice_rows, ff)], axis=2
        ),
        y, c, group,
    )
    g_att = dot(g_attn, w_out, NT).astype(BF16)
    dq, dk, dv, dkr, dvr = attend_back(q, kv, kv_rem, attended, g_att, plo, phi)
    far = swap_core(jnp.concatenate([dkr, dvr], axis=1)).astype(F32)
    g_mixed = jnp.concatenate(
        [dq, (dk + far[:, :feats]).astype(BF16), (dv + far[:, feats:]).astype(BF16)], axis=1
    )
    g_first = dot(g_mixed, w_qkv, NT)
    _, first_pull = jax.vjp(norm_rows, tokens, ga, sa)
    g_tok, g_ga, g_sa = first_pull(g_first)
    g_inputs = swap_out((g_res + g_tok).astype(BF16)).astype(F32)
    gw_qkv = dot(first, g_mixed, TN).astype(BF16)
    mixed_sums = jnp.sum(g_mixed.astype(F32), axis=0)
    vec_grads = (
        g_ga, g_sa, jnp.concatenate([mixed_sums[:feats], mixed_sums[2 * feats :]]),
        jnp.sum(g_attn.astype(F32), axis=0), g_gm, g_sm,
        jnp.sum(g_pre.astype(F32), axis=0), jnp.sum(g_final.astype(F32), axis=0),
    )
    vec_pack = jnp.concatenate([v.reshape(4, -1) for v in vec_grads], axis=1)
    vec_pack = jnp.pad(vec_pack, ((0, 0), (0, rows_v * width - vec_pack.shape[1])))
    vec_pack = vec_pack.reshape(4, rows_v, width).astype(BF16)
    step = 2 * groups
    pad = -(slice_rows + rows_v) % step
    vec_pack = jnp.pad(vec_pack, ((0, 0), (0, pad), (0, 0)))
    own_last = reduce_all(
        jnp.concatenate([gw_qkv.reshape(4, slice_rows, width), vec_pack], axis=1), y, c, group
    )
    own_qkv = own_last[:slice_rows]
    own_vec = own_last[slice_rows : slice_rows + rows_v].reshape(-1) * grad_factor
    vecs = []
    at = 0
    for size in sizes:
        vecs.append(own_vec[at : at + size])
        at += size
    own_mid = own_mid * grad_factor
    return (
        outputs, g_inputs, vecs[0], vecs[1], own_qkv * grad_factor, vecs[2],
        own_mid[:, :feats], vecs[3], vecs[4], vecs[5], own_mid[:, feats:], vecs[6],
        own_down * grad_factor, vecs[7],
    )


def solution(mesh):
    row = P("shard", None)
    vec = P("shard")
    big = P(None, "group", "shard", None)
    in_specs = (
        big, P(None, "group", None), vec, vec, row, vec, row, vec, vec, vec, row, vec, row, vec, big,
    )
    out_specs = (big, big, vec, vec, row, vec, row, vec, vec, vec, row, vec, row, vec)
    return jax.shard_map(body, mesh=mesh, in_specs=in_specs, out_specs=out_specs, check_vma=False)
```

```python
import functools
import math

import jax
import jax.numpy as jnp
from jax import lax
from jax.experimental import pallas as pl
from jax.experimental.pallas import tpu as pltpu
from jax.sharding import PartitionSpec as P

DEPTH = 48
PAIR = 128
NN = (((1,), (0,)), ((), ()))
NT = (((1,), (1,)), ((), ()))
TN = (((0,), (0,)), ((), ()))
F32 = jnp.float32
BF16 = jnp.bfloat16
VMEM = pl.BlockSpec(memory_space=pltpu.VMEM)
HBM = pl.BlockSpec(memory_space=pl.ANY)
BRANCH = 1.0 / math.sqrt(DEPTH)
EPS = 1e-05


def dot(a, b, dims):
    return lax.dot_general(a, b, dims, preferred_element_type=F32)


def shape(dims, dtype):
    return jax.ShapeDtypeStruct(dims, dtype)


def call(kernel, name, ins, outs, scratch, args, flops, mib):
    moved = sum(math.prod(a.shape) * a.dtype.itemsize for a in args)
    moved += sum(math.prod(o.shape) * o.dtype.itemsize for _, o in outs)
    return pl.pallas_call(
        kernel,
        in_specs=ins,
        out_specs=[spec for spec, _ in outs],
        out_shape=[o for _, o in outs],
        scratch_shapes=scratch,
        compiler_params=pltpu.CompilerParams(vmem_limit_bytes=mib << 20),
        cost_estimate=pl.CostEstimate(flops=flops, transcendentals=0, bytes_accessed=moved),
        name=name,
    )(*args)


def swap_core(x):
    return lax.ppermute(x, "shard", [(s, s ^ 1) for s in range(4)])


def swap_y(x):
    return lax.ppermute(x, "shard", [(s, s ^ 2) for s in range(4)])


def swap_group(x, bit):
    n = lax.axis_size("group")
    return lax.ppermute(x, "group", [(g, g ^ bit) for g in range(n)])


def tie(x, *others):
    return lax.optimization_barrier((x,) + others)[0]


def pick(x, index, axis):
    return lax.dynamic_index_in_dim(x, index, axis, keepdims=False)


def halves(x, index):
    rows = x.shape[0] // 2
    keep = lax.dynamic_slice_in_dim(x, index * rows, rows, 0)
    send = lax.dynamic_slice_in_dim(x, (1 - index) * rows, rows, 0)
    return keep, send


def add_low(*terms):
    total = terms[0].astype(F32)
    for term in terms[1:]:
        total = total + term.astype(F32)
    return total.astype(BF16)


class Order:
    def __init__(self):
        self.waiting = []
        self.last = None

    def need(self, x):
        self.waiting.append(x)
        return x

    def late(self, x):
        return x if self.last is None else tie(x, self.last)

    def run(self, stage, first, *rest):
        others = self.waiting + ([] if self.last is None else [self.last])
        outs = stage(tie(first, *others) if others else first, *rest)
        self.waiting = []
        self.last = outs[0]
        return outs


class Chain:
    def __init__(self, order, group):
        n = lax.axis_size("group")
        bits = [1 << i for i in range(n.bit_length() - 1)]
        self.plan = [("out", b) for b in bits[:-1]] + [("all", b) for b in bits[-1:]]
        self.plan += [("in", b) for b in reversed(bits[:-1])]
        self.order, self.group, self.at = order, group, 0
        self.held = self.recv = None

    def begin(self, held):
        self.held = held
        self.send()

    def send(self):
        if self.at == len(self.plan):
            return
        kind, bit = self.plan[self.at]
        if kind == "out":
            self.held, out = halves(self.held, (self.group // bit) % 2)
        else:
            out = self.held
        self.recv = swap_group(self.order.need(out), bit)

    def step(self):
        if self.at == len(self.plan):
            return
        kind, bit = self.plan[self.at]
        recv = self.order.late(self.recv)
        if kind == "in":
            self.held = jnp.where(
                (self.group // bit) % 2 == 0,
                jnp.concatenate([self.held, recv], axis=0),
                jnp.concatenate([recv, self.held], axis=0),
            )
        else:
            self.held = add_low(self.held, recv)
        self.at += 1
        self.send()

    def finish(self):
        while self.at < len(self.plan):
            self.step()
        return self.held


def place():
    s = lax.axis_index("shard")
    return s, s // 2


def spots(s, xb, rows):
    h = rows // 2
    far, both_far = (s ^ 2) * rows, (s ^ 3) * rows
    return (
        s * rows, (s ^ 1) * rows, far + xb * h, far + (1 - xb) * h, both_far + xb * h, both_far + (1 - xb) * h,
    )


def load_pieces(pieces, target, sems, cols=None):
    s, _ = place()
    xb = lax.axis_index("group") % 2
    copies = []
    if len(pieces) == 4:
        places = [(s ^ k) * pieces[0].shape[0] for k in range(4)]
    else:
        places = spots(s, xb, pieces[0].shape[0])
    for k, at in enumerate(places):
        source = pieces[k] if cols is None else pieces[k].at[:, cols[k]]
        spot = pl.ds(pl.multiple_of(at, 8), pieces[k].shape[0])
        copies.append(pltpu.make_async_copy(source, target.at[spot, :], sems.at[k]))
    return copies


def run_all(copies):
    for copy in copies:
        copy.start()
    return copies


def store_pieces(source, keep, send, sems, s):
    rows = keep.shape[1]
    copies = []
    for k, target in enumerate((keep.at[0], send.at[0], keep.at[1], send.at[1])):
        spot = pl.multiple_of((s ^ k) * rows, 8)
        copy = pltpu.make_async_copy(source.at[pl.ds(spot, rows), :], target, sems.at[k])
        copy.start()
        copies.append(copy)
    return copies


def stats(rows):
    center = jnp.mean(rows, axis=1, keepdims=True)
    deviate = rows - center
    scale = lax.rsqrt(jnp.mean(deviate * deviate, axis=1, keepdims=True) + EPS)
    return deviate * scale, scale


def norm_back(grad, normal, scale, gain):
    g = grad * gain
    return (g - jnp.mean(g, axis=1, keepdims=True) - normal * jnp.mean(g * normal, axis=1, keepdims=True)) * scale


def both(own_ref, oth_ref, y):
    blk = own_ref.shape[0]
    return (
        (own_ref, pl.ds(pl.multiple_of(y * blk, blk), blk)),
        (oth_ref, pl.ds(pl.multiple_of((1 - y) * blk, blk), blk)),
    )


def open_kernel(own, oth, ga, sa, bias, w0, w1, w2, w3, w4, w5, first, q, kv, w, sems):
    s, y = place()
    copies = run_all(load_pieces((w0, w1, w2, w3, w4, w5), w, sems))
    for ref, span in both(own, oth, y):
        normal, _ = stats(ref[...].astype(F32))
        first[span, :] = (normal * ga[...] + sa[...]).astype(BF16)
    for copy in copies:
        copy.wait()
    d = first.shape[1]
    f = first[...]
    q[...] = (dot(f, w[:, 0:d], NN) + bias[:, 0:d]).astype(BF16)
    kv[:, 0:d] = dot(f, w[:, d : 2 * d], NN).astype(BF16)
    kv[:, d:] = (dot(f, w[:, 2 * d :], NN) + bias[:, d:]).astype(BF16)


def open_stage(own, oth, ga, sa, bias, pieces):
    rows, d = 2 * own.shape[0], own.shape[1]
    width = pieces[0].shape[1]
    return call(
        open_kernel, "k_open", [VMEM] * 5 + [HBM] * 6,
        [(VMEM, shape((rows, d), BF16)), (VMEM, shape((rows, d), BF16)), (VMEM, shape((rows, 2 * d), BF16))],
        [pltpu.VMEM((d, width), BF16), pltpu.SemaphoreType.DMA((6,))],
        (own, oth, ga, sa, bias, *pieces), 2 * rows * d * width, 14,
    )


def middle_kernel(att_a, att_b, own, oth, bo, gm, sm, w0, w1, w2, w3, residual, second, w, sems):
    s, y = place()
    for copy in run_all(load_pieces((w0, w1, w2, w3), w, sems)):
        copy.wait()
    cut = att_a.shape[1]
    for ref, span in both(own, oth, y):
        mixed = dot(att_a[span, :], w[0:cut, :], NN) + dot(att_b[span, :], w[cut:, :], NN)
        res = ref[...].astype(F32) + BRANCH * (mixed + bo[...])
        residual[span, :] = res
        normal, _ = stats(res)
        second[span, :] = (normal * gm[...] + sm[...]).astype(BF16)


def middle_stage(att_a, att_b, own, oth, bo, gm, sm, pieces):
    rows, d = att_a.shape[0], own.shape[1]
    return call(
        middle_kernel, "k_middle", [VMEM] * 7 + [HBM] * 4,
        [(VMEM, shape((rows, d), F32)), (VMEM, shape((rows, d), BF16))],
        [pltpu.VMEM((d, d), BF16), pltpu.SemaphoreType.DMA((4,))],
        (att_a, att_b, own, oth, bo, gm, sm, *pieces), 2 * rows * d * d, 12,
    )


def down_block(k, pieces, target, sems):
    if k < 2:
        return [pltpu.make_async_copy(pieces[k], target, sems.at[0])]
    xb = lax.axis_index("group") % 2
    h = pieces[2].shape[0]
    copies = []
    for i in range(2):
        at = xb * h if i == 0 else (1 - xb) * h
        spot = pl.ds(pl.multiple_of(at, 8), h)
        copies.append(pltpu.make_async_copy(pieces[2 * (k - 1) + i], target.at[spot, :], sems.at[i]))
    return copies


def final_kernel(own, oth, final, total_ref):
    _, y = place()
    total = None
    for ref, span in both(own, oth, y):
        g = (BRANCH * ref[...].astype(F32)).astype(BF16)
        final[span, :] = g
        part = jnp.sum(g.astype(F32), axis=0, keepdims=True)
        total = part if total is None else total + part
    total_ref[...] = total


def final_stage(own, oth):
    blk, d = own.shape
    return call(
        final_kernel, "k_final", [VMEM] * 2,
        [(VMEM, shape((2 * blk, d), BF16)), (VMEM, shape((1, d), F32))], [], (own, oth), blk * d, 8,
    )


def inner_kernel(
    k, fresh, second, final, bu, before, u0, u1, u2, u3, u4, u5, w0, w1, w2, w3, w4, w5,
    hidden, gpre, grad, sum_pre, after, up, down, upsem, downsem,
):
    s, _ = place()
    rows, d = second.shape
    blk = rows // 2
    cols = pl.ds(pl.multiple_of((s ^ k) * d, 128), d)
    ucopies = run_all(load_pieces((u0, u1, u2, u3, u4, u5), up, upsem, (cols,) * 6))
    dcopies = run_all(down_block(k, (w0, w1, w2, w3, w4, w5), down, downsem))
    for copy in ucopies + dcopies:
        copy.wait()
    bias = bu[:, cols]
    c0 = 0.7978845608028654
    c1 = c0 * 0.044715
    total = None
    for half in range(2):
        span = slice(half * blk, (half + 1) * blk)
        u = dot(second[span, :], up[...], NN) + bias
        gh = dot(final[span, :], down[...], NT)
        sq = u * u
        t = jnp.tanh(u * (c0 + c1 * sq))
        h = 0.5 + 0.5 * t
        value = u * h
        hidden[span, :] = value.astype(BF16)
        slope = h + value * (1.0 - t) * (c0 + 3.0 * c1 * sq)
        gp = (gh * slope).astype(BF16)
        gpre[span, :] = gp
        part = jnp.sum(gp.astype(F32), axis=0, keepdims=True)
        total = part if total is None else total + part
        t = dot(gp, up[...], NT)
        after[span, :] = t if fresh else before[span, :] + t
    sum_pre[...] = total
    grad[...] = dot(hidden[...], final[...], TN).astype(BF16)


def inner_stage(k, fresh, second, final, bu, before, ups, downs):
    rows, d = second.shape
    return call(
        functools.partial(inner_kernel, k, fresh), "k_inner", [VMEM] * 4 + [HBM] * 12,
        [
            (VMEM, shape((rows, d), BF16)), (VMEM, shape((rows, d), BF16)),
            (VMEM, shape((d, d), BF16)), (VMEM, shape((1, d), F32)), (VMEM, shape((rows, d), F32)),
        ],
        [
            pltpu.VMEM((d, d), BF16), pltpu.VMEM((d, d), BF16),
            pltpu.SemaphoreType.DMA((6,)), pltpu.SemaphoreType.DMA((2,)),
        ],
        (second, final, bu, before, *ups, *downs), 8 * rows * d * d, 24,
    )


def lower_kernel(
    second_grad, residual, own, oth, gm, o0, o1, o2, o3,
    g_att, g_res, attn, sum_gm, sum_sm, sum_attn, wo, osem,
):
    _, y = place()
    ocopies = run_all(load_pieces((o0, o1, o2, o3), wo, osem))
    t_gm = t_sm = t_at = None
    for i, (ref, span) in enumerate(both(own, oth, y)):
        normal, scale = stats(residual[span, :])
        g2 = second_grad[span, :]
        res = ref[...].astype(F32) + norm_back(g2, normal, scale, gm[...])
        g_res[span, :] = res
        ga = (BRANCH * res).astype(BF16)
        attn[span, :] = ga
        parts = (
            jnp.sum(g2 * normal, axis=0, keepdims=True),
            jnp.sum(g2, axis=0, keepdims=True),
            jnp.sum(ga.astype(F32), axis=0, keepdims=True),
        )
        if i == 0:
            t_gm, t_sm, t_at = parts
            for copy in ocopies:
                copy.wait()
        else:
            t_gm, t_sm, t_at = t_gm + parts[0], t_sm + parts[1], t_at + parts[2]
        g_att[span, :] = dot(ga, wo[...], NT).astype(BF16)
    sum_gm[...] = t_gm
    sum_sm[...] = t_sm
    sum_attn[...] = t_at


def lower_stage(second_grad, residual, own, oth, gm, outs):
    rows, d = residual.shape
    vec = (VMEM, shape((1, d), F32))
    return call(
        lower_kernel, "k_lower", [VMEM] * 5 + [HBM] * 4,
        [(VMEM, shape((rows, d), BF16)), (VMEM, shape((rows, d), F32)), (VMEM, shape((rows, d), BF16)), vec, vec, vec],
        [pltpu.VMEM((d, d), BF16), pltpu.SemaphoreType.DMA((4,))],
        (second_grad, residual, own, oth, gm, *outs), 2 * rows * d * d, 16,
    )


def up_grad_kernel(chunk, second, p0, p1, p2, p3, *rest):
    extra, (keep, send, grad, sems) = rest[:-4], rest[-4:]
    s, y = place()
    c = s % 2
    d = second.shape[1]
    for side, refs in enumerate(((p0, p1), (p2, p3))):

        @pl.when(y == (chunk ^ side))
        def _(refs=refs):
            for i, ref in enumerate(refs):
                cols = pl.ds(pl.multiple_of((c ^ i) * d, 128), d)
                grad[:, cols] = dot(second[...], ref[...], TN).astype(BF16)

    if extra:
        att_a, att_b, attn = extra
        cut = att_a.shape[1]
        grad[0:cut, 2 * d :] = dot(att_a[...], attn[...], TN).astype(BF16)
        grad[cut:, 2 * d :] = dot(att_b[...], attn[...], TN).astype(BF16)
    for copy in store_pieces(grad, keep, send, sems, s):
        copy.wait()


def up_grad_stage(chunk, second, gpres, extra=()):
    rows, d = second.shape
    r = d // 4
    wide = (3 if extra else 2) * d
    return call(
        functools.partial(up_grad_kernel, chunk), "k_up_grad", [VMEM] * (5 + len(extra)),
        [(HBM, shape((2, r, wide), BF16)), (HBM, shape((2, r, wide), BF16))],
        [pltpu.VMEM((d, wide), BF16), pltpu.SemaphoreType.DMA((4,))],
        (second, *gpres, *extra), 2 * rows * d * wide, 16,
    )


def close_kernel(count, *refs):
    groups = [refs[3 * i : 3 * i + 3] for i in range(count)]
    first, mixed, keep, send, sums, grad, sems = refs[3 * count :]
    s, _ = place()
    w = groups[0][0].shape[1]
    for g, (dq, own, far) in enumerate(groups):
        mixed[:, g * w : (g + 1) * w] = dq[...]
        for i in range(2):
            total = own[i] + far[i].astype(F32)
            at = ((i + 1) * count + g) * w
            mixed[:, at : at + w] = total.astype(BF16)
    for i in range(3):
        cols = slice(i * count * w, (i + 1) * count * w)
        part = mixed[:, cols]
        sums[:, cols] = jnp.sum(part.astype(F32), axis=0, keepdims=True)
        grad[:, cols] = dot(first[...], part, TN).astype(BF16)
    for copy in store_pieces(grad, keep, send, sems, s):
        copy.wait()


def close_stage(*args):
    first = args[-1]
    count = len(args) // 3
    rows, d = first.shape
    w = 3 * count * args[0].shape[1]
    r = d // 4
    return call(
        functools.partial(close_kernel, count), "k_close", [VMEM] * len(args),
        [
            (VMEM, shape((rows, w), BF16)), (HBM, shape((2, r, w), BF16)),
            (HBM, shape((2, r, w), BF16)), (VMEM, shape((1, w), F32)),
        ],
        [pltpu.VMEM((d, w), BF16), pltpu.SemaphoreType.DMA((4,))],
        args, 2 * rows * d * w, 16,
    )


def input_kernel(
    mixed_a, mixed_b, own, oth, ga, g_res, mix_a, mix_b, s_at, s_gm, s_sm, q0, q1, q2, q3, s_fin,
    w0, w1, w2, w3, w4, w5, keep, send, sums, w, sems,
):
    s, y = place()
    copies = run_all(load_pieces((w0, w1, w2, w3, w4, w5), w, sems))
    d = own.shape[1]
    wa, wb = mixed_a.shape[1] // 3, mixed_b.shape[1] // 3
    sums[2:3, 0:wa] = mix_a[:, 0:wa]
    sums[2:3, wa:] = mix_b[:, 0:wb]
    sums[3:4, 0:wa] = mix_a[:, 2 * wa :]
    sums[3:4, wa:] = mix_b[:, 2 * wb :]
    sums[4:5, :] = s_at[...]
    sums[5:6, :] = s_gm[...]
    sums[6:7, :] = s_sm[...]
    for k, ref in enumerate((q0, q1, q2, q3)):
        sums[pl.ds(7 + (s ^ k), 1), :] = ref[...]
    sums[11:12, :] = s_fin[...]
    for copy in copies:
        copy.wait()
    t_ga = t_sa = None
    for i, (ref, span) in enumerate(both(own, oth, y)):
        g = None
        for at, wide, mixed in ((0, wa, mixed_a), (wa, wb, mixed_b)):
            for part in range(3):
                spot = part * d + at
                t = dot(mixed[span, part * wide : (part + 1) * wide], w[:, spot : spot + wide], NT)
                g = t if g is None else g + t
        normal, scale = stats(ref[...].astype(F32))
        grad = g_res[span, :] + norm_back(g, normal, scale, ga[...])
        if i == 0:
            keep[...] = grad
        else:
            send[...] = grad.astype(BF16)
        parts = jnp.sum(g * normal, axis=0, keepdims=True), jnp.sum(g, axis=0, keepdims=True)
        t_ga = parts[0] if t_ga is None else t_ga + parts[0]
        t_sa = parts[1] if t_sa is None else t_sa + parts[1]
    sums[0:1, :] = t_ga
    sums[1:2, :] = t_sa


def input_stage(mixed_a, mixed_b, own, oth, ga, g_res, vecs, pieces):
    blk, d = own.shape
    return call(
        input_kernel, "k_input", [VMEM] * (6 + len(vecs)) + [HBM] * 6,
        [(VMEM, shape((blk, d), F32)), (VMEM, shape((blk, d), BF16)), (VMEM, shape((12, d), F32))],
        [pltpu.VMEM((d, 3 * d), BF16), pltpu.SemaphoreType.DMA((6,))],
        (mixed_a, mixed_b, own, oth, ga, g_res, *vecs, *pieces), 12 * blk * d * d, 16,
    )


def output_kernel(h0, h1, h2, h3, residual, bd, w0, w1, w2, w3, w4, w5, keep, send, w, sems):
    _, y = place()
    blk = keep.shape[0]
    copies = [run_all(down_block(k, (w0, w1, w2, w3, w4, w5), w.at[k], sems.at[k])) for k in range(4)]
    for group in copies:
        for copy in group:
            copy.wait()
    for i, out in enumerate((keep, send)):
        at = y if i == 0 else 1 - y
        span = pl.ds(pl.multiple_of(at * blk, blk), blk)
        total = None
        for k, ref in enumerate((h0, h1, h2, h3)):
            t = dot(ref[span, :], w[k], NN)
            total = t if total is None else total + t
        out[...] = (residual[span, :] + BRANCH * (total + bd[...])).astype(BF16)


def output_stage(h0, h1, h2, h3, residual, bd, downs):
    rows, d = residual.shape
    return call(
        output_kernel, "k_output", [VMEM] * 6 + [HBM] * 6,
        [(VMEM, shape((rows // 2, d), BF16)), (VMEM, shape((rows // 2, d), BF16))],
        [pltpu.VMEM((4, d, d), BF16), pltpu.SemaphoreType.DMA((4, 2))],
        (h0, h1, h2, h3, residual, bd, *downs), 8 * rows * d * d, 16,
    )


def bias_of(qid, kid):
    return jnp.where(kid <= qid, 0.0, -1e30).astype(F32)


def column(row):
    n = row.shape[1]
    return jnp.transpose(jnp.broadcast_to(row, (PAIR, n)))[:, 0:1]


def head_lanes(dims, head):
    lane = lax.broadcasted_iota(jnp.int32, dims, len(dims) - 1)
    return (lane < 64) if head == 0 else (lane >= 64)


def attend_kernel(ids_ref, q_ref, k_ref, kr_ref, v_ref, vr_ref, o_ref, plo_ref, phi_ref, blo, bhi):
    blk = q_ref.shape[0] // 2

    @pl.when(pl.program_id(0) == 0)
    def _():
        s, y = place()
        c = s % 2
        ids = ids_ref[y].astype(F32)
        chunks = [ids[:, j * blk : (j + 1) * blk] for j in range(4)]
        even = c == 0
        own0, own1 = jnp.where(even, chunks[0], chunks[1]), jnp.where(even, chunks[2], chunks[3])
        rem0, rem1 = jnp.where(even, chunks[1], chunks[0]), jnp.where(even, chunks[3], chunks[2])
        q0, q1 = column(own0), column(own1)
        blo[...] = jnp.concatenate([bias_of(q0, k) for k in (own0, rem0, rem1)], axis=1)
        bhi[...] = jnp.concatenate([bias_of(q1, k) for k in (own0, rem0, rem1, own1)], axis=1)

    keys = [k_ref[0:blk, :], kr_ref[0:blk, :], kr_ref[blk:, :], k_ref[blk:, :]]
    vals = [v_ref[0:blk, :], vr_ref[0:blk, :], vr_ref[blk:, :], v_ref[blk:, :]]
    for half, (bias, count, p_ref) in enumerate(((blo, 3, plo_ref), (bhi, 4, phi_ref))):
        q = q_ref[half * blk : (half + 1) * blk, :] * BF16(0.125)
        outs = []
        for head in range(2):
            qh = jnp.where(head_lanes(q.shape, head), q, BF16(0))
            s = jnp.concatenate([dot(qh, keys[j], NT) for j in range(count)], axis=1) + bias[...]
            e = jnp.exp(s - jnp.max(s, axis=1, keepdims=True))
            p = (e * (1.0 / jnp.sum(e, axis=1, keepdims=True))).astype(BF16)
            p_ref[head] = p
            acc = None
            for j in range(count):
                t = dot(p[:, j * blk : (j + 1) * blk], vals[j], NN)
                acc = t if acc is None else acc + t
            outs.append(acc)
        o = jnp.where(head_lanes(outs[0].shape, 0), outs[0], outs[1])
        o_ref[half * blk : (half + 1) * blk, :] = o.astype(BF16)


def attend(lo, hi, q, kv, kv_rem, ids):
    rows, feats = q.shape
    blk = rows // 2
    pairs = feats // PAIR
    n = hi - lo
    col = lambda off: pl.BlockSpec((rows, PAIR), lambda i, off=off: (0, i + off))
    return pl.pallas_call(
        attend_kernel,
        grid=(n,),
        in_specs=[
            pl.BlockSpec(ids.shape, lambda i: (0, 0, 0)),
            col(lo), col(lo), col(lo), col(pairs + lo), col(pairs + lo),
        ],
        out_specs=[
            col(0),
            pl.BlockSpec((2, blk, 3 * blk), lambda i: (i, 0, 0)),
            pl.BlockSpec((2, blk, 4 * blk), lambda i: (i, 0, 0)),
        ],
        out_shape=[
            shape((rows, n * PAIR), BF16),
            shape((2 * n, blk, 3 * blk), BF16),
            shape((2 * n, blk, 4 * blk), BF16),
        ],
        scratch_shapes=[pltpu.VMEM((blk, 3 * blk), F32), pltpu.VMEM((blk, 4 * blk), F32)],
        compiler_params=pltpu.CompilerParams(vmem_limit_bytes=20 << 20),
        cost_estimate=pl.CostEstimate(
            flops=4 * 7 * blk * blk * n * PAIR * 4, transcendentals=7 * blk * blk * 2 * n, bytes_accessed=3 * n << 20
        ),
        name="k_attend",
    )(ids, q, kv, kv_rem, kv, kv_rem)


def attend_back_kernel(
    q_ref, k_ref, kr_ref, v_ref, vr_ref, o_ref, g_ref, plo_ref, phi_ref,
    dq_ref, own_ref, far_ref, acc_k, acc_v,
):
    blk = q_ref.shape[0] // 2
    keys = [k_ref[0:blk, :], kr_ref[0:blk, :], kr_ref[blk:, :], k_ref[blk:, :]]
    vals = [v_ref[0:blk, :], vr_ref[0:blk, :], vr_ref[blk:, :], v_ref[blk:, :]]
    for half, (count, p_ref) in enumerate(((3, plo_ref), (4, phi_ref))):
        span = slice(half * blk, (half + 1) * blk)
        q = q_ref[span, :] * BF16(0.125)
        g = g_ref[span, :]
        og = o_ref[span, :].astype(F32) * g.astype(F32)
        dqs = []
        terms_k = [[] for _ in range(count)]
        terms_v = [[] for _ in range(count)]
        for head in range(2):
            lanes = head_lanes(q.shape, head)
            gh = jnp.where(lanes, g, BF16(0))
            inner = jnp.sum(jnp.where(lanes, og, 0.0), axis=1, keepdims=True)
            acc = None
            for j in range(count):
                p = p_ref[head, :, j * blk : (j + 1) * blk]
                dp = dot(gh, vals[j], NT)
                ds = (p.astype(F32) * (dp - inner)).astype(BF16)
                t = dot(ds, keys[j], NN)
                acc = t if acc is None else acc + t
                terms_k[j].append(dot(ds, q, TN))
                terms_v[j].append(dot(p, g, TN))
            dqs.append(acc)
        lanes = head_lanes(dqs[0].shape, 0)
        dq_ref[span, :] = (jnp.where(lanes, dqs[0], dqs[1]) * 0.125).astype(BF16)
        for j in range(count):
            spot = slice(j * blk, (j + 1) * blk)
            tk = jnp.where(lanes, terms_k[j][0], terms_k[j][1])
            tv = jnp.where(lanes, terms_v[j][0], terms_v[j][1])
            if half == 0:
                acc_k[spot, :] = tk
                acc_v[spot, :] = tv
            elif j == 3:
                own_ref[0, blk:, :] = tk
                own_ref[1, blk:, :] = tv
            else:
                tk = acc_k[spot, :] + tk
                tv = acc_v[spot, :] + tv
                if j == 0:
                    own_ref[0, 0:blk, :] = tk
                    own_ref[1, 0:blk, :] = tv
                else:
                    spot = slice((j - 1) * blk, j * blk)
                    far_ref[0, spot, :] = tk.astype(BF16)
                    far_ref[1, spot, :] = tv.astype(BF16)


def attend_back(lo, hi, base, g, q, kv, kv_rem, o, plo, phi):
    rows, feats = q.shape
    blk = rows // 2
    pairs = feats // PAIR
    n = hi - lo
    col = lambda off: pl.BlockSpec((rows, PAIR), lambda i, off=off: (0, i + off))
    two = pl.BlockSpec((2, rows, PAIR), lambda i: (0, 0, i))
    wide = n * PAIR
    return pl.pallas_call(
        attend_back_kernel,
        grid=(n,),
        in_specs=[
            col(lo), col(lo), col(lo), col(pairs + lo), col(pairs + lo), col(lo - base), col(lo),
            pl.BlockSpec((2, blk, 3 * blk), lambda i: (i + lo - base, 0, 0)),
            pl.BlockSpec((2, blk, 4 * blk), lambda i: (i + lo - base, 0, 0)),
        ],
        out_specs=[col(0), two, two],
        out_shape=[shape((rows, wide), BF16), shape((2, rows, wide), F32), shape((2, rows, wide), BF16)],
        scratch_shapes=[pltpu.VMEM((3 * blk, PAIR), F32), pltpu.VMEM((3 * blk, PAIR), F32)],
        compiler_params=pltpu.CompilerParams(vmem_limit_bytes=20 << 20),
        cost_estimate=pl.CostEstimate(
            flops=8 * 7 * blk * blk * wide * 4, transcendentals=0, bytes_accessed=4 * n << 20
        ),
        name="k_attend_back",
    )(q, kv, kv_rem, kv, kv_rem, o, g, plo, phi)


def body(
    inputs, block_ids, attn_gain, attn_shift, weight_qkv, bias_qv, weight_out, bias_out,
    mlp_gain, mlp_shift, weight_up, bias_up, weight_down, bias_down, cotangent,
):
    micro_count, seq_count, blk, feats = inputs.shape
    seq_length = block_ids.shape[2]
    shard = lax.axis_index("shard")
    group = lax.axis_index("group")
    groups = lax.axis_size("group")
    y, c = shard // 2, shard % 2
    grad_factor = 1.0 / math.sqrt(micro_count * seq_count * seq_length * groups)

    xb = group % 2
    half_of = lambda w: lax.dynamic_slice_in_dim(w, xb * (w.shape[0] // 2), w.shape[0] // 2, 0)

    order = Order()
    need, late, run = order.need, order.late, order.run

    qkv_near = swap_y(half_of(weight_qkv))
    x_own = pick(inputs, y, 0)[0]
    x_oth = swap_y(pick(inputs, 1 - y, 0)[0])
    qkv_core = swap_core(weight_qkv)
    vectors = (attn_gain, attn_shift, bias_qv, bias_out, mlp_gain, mlp_shift, bias_up, bias_down)
    sizes = [v.shape[0] for v in vectors]
    packed = jnp.concatenate(vectors)
    p2 = swap_y(packed)
    p0, p1, p3 = packed, swap_core(packed), swap_core(p2)
    qkv_over = swap_group(qkv_near, 1)
    wout_far = swap_y(tie(weight_out, qkv_near))
    up_half = tie(half_of(weight_up), qkv_near)
    up_near = swap_y(up_half)
    qkvs = [weight_qkv, qkv_core, qkv_near, qkv_over, swap_core(qkv_near), swap_core(qkv_over)]
    even = c == 0
    a0, a1 = jnp.where(even, p0, p1), jnp.where(even, p1, p0)
    a2, a3 = jnp.where(even, p2, p3), jnp.where(even, p3, p2)
    front = y == 0
    vec_rows = jnp.stack(
        [jnp.where(front, a0, a2), jnp.where(front, a1, a3), jnp.where(front, a2, a0), jnp.where(front, a3, a1)]
    ).astype(F32)
    full = []
    at = 0
    for size in sizes:
        full.append(need(vec_rows[:, at : at + size].reshape(1, 4 * size)))
        at += size
    ga, sa, bqv, bo, gm, sm, bu, bd = full
    need(up_half)

    first, q, kv = run(open_stage, x_own, x_oth, ga, sa, bqv, qkvs)
    kv_rem = swap_core(kv)
    up_near = late(up_near)
    up_over = swap_group(need(up_near), 1)
    wout_core = swap_core(weight_out)
    wout_far = late(wout_far)
    wout_both = swap_core(wout_far)
    down_half = need(late(half_of(weight_down)))
    down_near = swap_y(down_half)
    g_send = need(late(pick(cotangent, 1 - y, 0)[0]))
    g_oth = swap_y(g_send)
    g_own = pick(cotangent, y, 0)[0]
    pairs = feats // PAIR
    p_a, p_b = pairs // 3, 2 * pairs // 3
    att_a, plo_a, phi_a = run(functools.partial(attend, 0, p_a), q, kv, kv_rem, block_ids)
    up_core, up_both = swap_core(late(weight_up)), swap_core(late(up_near))
    att_b, plo_b, phi_b = run(functools.partial(attend, p_a, pairs), q, kv, kv_rem, block_ids)
    down_near = need(late(down_near))
    down_over = swap_group(down_near, 1)
    down_core, down_both = swap_core(late(weight_down)), swap_core(down_near)
    up_over = need(late(up_over))
    ups = [weight_up, up_core, up_near, up_over, up_both, swap_core(up_over)]
    residual, second = run(
        middle_stage, att_a, att_b, x_own, x_oth, bo, gm, sm, [weight_out, wout_core, wout_far, wout_both]
    )
    final, sum_final = run(final_stage, late(g_own), g_oth)
    down_over = late(down_over)
    downs = [weight_down, down_core, down_near, down_over, down_both, swap_core(down_over)]

    hidden, gpre, gdown, sum_pre = [None] * 4, [None] * 4, [None] * 4, [None] * 4
    acc = residual
    down_chain, mid_chain_a, mid_chain_b = Chain(order, group), Chain(order, group), Chain(order, group)
    for k in (3, 2, 1, 0):
        hidden[k], gpre[k], gdown[k], sum_pre[k], acc = run(
            functools.partial(inner_stage, k, k == 3), second, final, bu, acc, ups, downs
        )
        if k == 3:
            recv3 = swap_core(need(gdown[3]))
        if k == 2:
            down_y = swap_y(need(add_low(gdown[2], late(recv3))))
        if k == 1:
            recv1 = swap_core(need(gdown[1]))
    wouts = [weight_out, wout_core, wout_far, wout_both]
    g_att, g_res, attn, sum_gm, sum_sm, sum_attn = run(lower_stage, acc, residual, g_own, g_oth, gm, wouts)
    keep_a, send_a = run(functools.partial(up_grad_stage, 0), second, gpre)
    recv_a = swap_core(need(send_a))
    keep_b, send_b = run(functools.partial(up_grad_stage, 1), second, gpre, (att_a, att_b, attn))
    recv_b = swap_core(need(send_b))
    recv_a = late(recv_a)
    mid_ya = swap_y(need(add_low(keep_a[1], recv_a[1])))

    dq1, own1, far1 = run(functools.partial(attend_back, 0, p_a, 0), g_att, q, kv, kv_rem, att_a, plo_a, phi_a)
    recv_b = late(recv_b)
    mid_yb = swap_y(need(add_low(keep_b[1], recv_b[1])))
    down_chain.begin(add_low(gdown[0], late(recv1), late(down_y)))
    far1 = swap_core(need(far1))
    dq2, own2, far2 = run(functools.partial(attend_back, p_a, p_b, p_a), g_att, q, kv, kv_rem, att_b, plo_b, phi_b)
    mid_chain_a.begin(add_low(keep_a[0], recv_a[0], late(mid_ya)))
    far2 = swap_core(need(far2))
    dq3, own3, far3 = run(functools.partial(attend_back, p_b, pairs, p_a), g_att, q, kv, kv_rem, att_b, plo_b, phi_b)
    far3 = swap_core(need(far3))
    down_chain.step()
    mid_chain_a.step()
    mid_chain_b.begin(add_low(keep_b[0], recv_b[0], late(mid_yb)))
    mixed_a, keep_c, send_c, mix_a = run(close_stage, dq1, own1, late(far1), dq2, own2, late(far2), first)
    recv_c = swap_core(need(send_c))
    down_chain.step()
    mid_chain_a.step()
    mixed_b, keep_d, send_d, mix_b = run(close_stage, dq3, own3, late(far3), first)
    recv_d = swap_core(need(send_d))
    recv_c = late(recv_c)
    y_c = swap_y(need(add_low(keep_c[1], recv_c[1])))
    mid_chain_b.step()
    vecs = (mix_a, mix_b, sum_attn, sum_gm, sum_sm, *sum_pre, sum_final)
    gin_keep, gin_send, sums = run(input_stage, mixed_a, mixed_b, x_own, x_oth, ga, g_res, vecs, qkvs)
    recv_d = late(recv_d)
    y_d = swap_y(need(add_low(keep_d[1], recv_d[1])))
    down_chain.step()
    mid_chain_a.step()
    gin_oth = swap_y(need(gin_send))
    sums_core = swap_core(need(sums))
    out_keep, out_send = run(output_stage, *hidden, residual, bd, downs)
    out_oth = swap_y(need(out_send))
    sums = sums + late(sums_core)
    chain_c, chain_d = Chain(order, group), Chain(order, group)
    sums = sums + swap_y(sums)
    chain_c.begin(add_low(keep_c[0], recv_c[0], late(y_c)))
    mid_chain_b.step()
    down_chain.step()
    mid_chain_a.step()
    chain_d.begin(add_low(keep_d[0], recv_d[0], late(y_d)))
    for i in range(groups.bit_length() - 1):
        sums = sums + swap_group(sums, 1 << i)
        chain_c.step()
        mid_chain_b.step()
        chain_d.step()
    own_down = down_chain.finish()
    own_a, own_b = mid_chain_a.finish(), mid_chain_b.finish()
    own_c, own_d = chain_c.finish(), chain_d.finish()

    def blocks(mine, other):
        other = other.astype(mine.dtype)
        return jnp.where(y == 0, jnp.stack([mine, other]), jnp.stack([other, mine]))[:, None]

    flat = sums.reshape(-1)
    vecs = []
    at = 0
    for size in sizes:
        vecs.append(lax.dynamic_slice(flat, (at + shard * size,), (size,)) * grad_factor)
        at += 4 * size
    scale = lambda v: v.astype(F32) * grad_factor
    wc, wd = own_c.shape[1] // 3, own_d.shape[1] // 3
    parts = []
    for i in range(3):
        parts += [own_c[:, i * wc : (i + 1) * wc], own_d[:, i * wd : (i + 1) * wd]]
    wide = own_a.shape[1]
    return (
        blocks(out_keep, out_oth), blocks(gin_keep, gin_oth), vecs[0], vecs[1],
        scale(jnp.concatenate(parts, axis=1)), vecs[2], scale(own_b[:, wide:]), vecs[3], vecs[4], vecs[5],
        scale(jnp.concatenate([own_a, own_b[:, :wide]], axis=1)), vecs[6], scale(own_down), vecs[7],
    )


def solution(mesh):
    row = P("shard", None)
    vec = P("shard")
    big = P(None, "group", "shard", None)
    in_specs = (
        big, P(None, "group", None), vec, vec, row, vec, row, vec, vec, vec, row, vec, row, vec, big,
    )
    out_specs = (big, big, vec, vec, row, vec, row, vec, vec, vec, row, vec, row, vec)
    return jax.shard_map(body, mesh=mesh, in_specs=in_specs, out_specs=out_specs, check_vma=False)
```
